256 devices in a mesh: seq: 32 (over y, z), head: 8 (over x, core).
Axes of the slice: x: 4, y: 4, z: 8, core: 2. Of those that a mesh axis runs over, the one named last changes fastest.
Arguments:
- query_input: bfloat16 [16384, 2048], P(('seq', 'head')), may hold values from -6 to 6
- key_input: bfloat16 [16384, 2048], P(('seq', 'head')), may hold values from -40 to 40
- value_input: bfloat16 [16384, 4096], P(('seq', 'head')), may hold values from -40 to 40
- gate_input: bfloat16 [16384, 4096], P(('seq', 'head')), may hold values from -6 to 6
- write_strength: bfloat16 [16384, 32], P(('seq', 'head')), may hold values from 0.0009 to 0.91
- log_decay: bfloat16 [16384, 32], P(('seq', 'head')), may hold values from -0.81 to 0
- filter_query: bfloat16 [4, 2048], P(None, 'head'), may hold values from -3 to 3
- filter_key: bfloat16 [4, 2048], P(None, 'head'), may hold values from -3 to 3
- filter_value: bfloat16 [4, 4096], P(None, 'head'), may hold values from -3 to 3
- norm_gain: float32 [128], replicated, may hold values from 0.1 to 1.9
- out_weight: bfloat16 [4096, 2048], P('head'), may hold values from -0.09375 to 0.09375
Outputs:
- stratum_result: bfloat16 [16384, 2048], P(('seq', 'head'))
The draws below stay inside these ranges and needn't reach their ends.
All inputs are finite; a program needn't handle non-finite values.
Results may differ from the reference program's by a relative error of at most 0.005.
Values may be sent and summed in bfloat16 or wider, within the bound.
A program may use at most 128 MiB of HBM per device.

```python
import math
import jax
import jax.numpy as jnp
from jax import lax

D = 2048
HK = 16
HV = 32
DK = 128
DV = 128
KW = 4
CH = 64
TOK_DEV = 512
L = 16384


def scaled_field(base_key, row_count, column_count):
    parts = jax.random.split(base_key, 3)
    base = jnp.clip(jax.random.normal(parts[0], (row_count, column_count), jnp.float32), -4.0, 4.0)
    column_scale = jnp.exp(jax.random.uniform(parts[1], (column_count,), jnp.float32, 0.0, math.log(10.0))) / math.sqrt(10.0)
    row_scale = jnp.exp(jax.random.uniform(parts[2], (row_count, 1), jnp.float32, 0.0, math.log(10.0))) / math.sqrt(10.0)
    return base * column_scale * row_scale


def head_layout(base_key):
    parts = jax.random.split(jax.random.fold_in(base_key, 21), 8)
    fast_share = 0.5
    fast_heads = jax.random.uniform(parts[0], (HV,), jnp.float32) < fast_share
    fast_rate = jnp.exp(jax.random.uniform(parts[1], (HV,), jnp.float32, math.log(1.0 / 40.0), math.log(1.0 / 15.0)))
    slow_rate = jnp.exp(jax.random.uniform(parts[2], (HV,), jnp.float32, math.log(0.05), math.log(0.3))) / L
    head_decay_speed = jnp.where(fast_heads, fast_rate, slow_rate)
    block_count = L // TOK_DEV
    block_factor = jnp.exp(jax.random.uniform(parts[3], (block_count, 1, HV), jnp.float32, math.log(0.5), math.log(2.0)))
    token_factor = jax.random.uniform(parts[4], (block_count, TOK_DEV, HV), jnp.float32, 0.5, 1.5)
    forgetting_rates = -(head_decay_speed * block_factor * token_factor).reshape(L, HV)
    flagged_locations = jax.random.randint(parts[5], (2, HV), 0, L)
    sequence_offsets = jnp.arange(L, dtype=jnp.int32)[:, None]
    spike_clusters = (sequence_offsets == flagged_locations[0][None, :]) | (sequence_offsets == flagged_locations[1][None, :])
    error_measures = jax.random.uniform(parts[6], (L, HV), jnp.float32, math.log(0.55), math.log(0.8))
    forgetting_rates = forgetting_rates + jnp.where(spike_clusters, error_measures, 0.0)
    strong = jax.random.uniform(parts[7], (L, HV), jnp.float32, 0.3, 0.9)
    weak = jnp.exp(jax.random.uniform(jax.random.fold_in(parts[7], 1), (L, HV), jnp.float32, math.log(0.001), math.log(0.003)))
    strength = jnp.where(fast_heads[None, :], strong, weak)
    return (forgetting_rates, strength)


def draw_key_input(key, part):
    return scaled_field(jax.random.fold_in(key, 11), L, HK * DK).astype(jnp.bfloat16)


def draw_value_input(key, part):
    return scaled_field(jax.random.fold_in(key, 12), L, HV * DV).astype(jnp.bfloat16)


def draw_write_strength(key, part):
    forgetting_rates, strength = head_layout(key)
    return strength.astype(jnp.bfloat16)


def draw_log_decay(key, part):
    forgetting_rates, strength = head_layout(key)
    return forgetting_rates.astype(jnp.bfloat16)


def block_levels(rng, dims, cuts, smallest, largest):
    level = 1.0
    for dim, blocks in cuts:
        draws = jax.random.uniform(jax.random.fold_in(jax.random.fold_in(rng, 6), dim), (blocks,), jnp.float32, smallest / len(cuts), largest / len(cuts))
        level = level * jnp.repeat(jnp.exp(draws), dims[dim] // blocks).reshape((-1,) + (1,) * (len(dims) - 1 - dim))
    return level


def normal_values(stream_key, shape, width, most, shards=(), kind=jnp.bfloat16):
    array = jax.random.normal(stream_key, shape, jnp.float32) * width
    if len(shards) > 0:
        array = block_levels(stream_key, shape, shards, -0.22, 0.18) * array
    return jnp.clip(array, min=-most, max=most).astype(kind)


def setup_inputs(seed: int = 0) -> dict:
    key_list = jax.random.split(jax.random.key(seed), 12)
    return {
        "query_input": normal_values(key_list[0], (L, HK * DK), 1.0, 6.0, ((0, 256),)),
        "key_input": draw_key_input(jax.random.fold_in(key_list[11], 71), 0),
        "value_input": draw_value_input(jax.random.fold_in(key_list[11], 71), 0),
        "gate_input": normal_values(key_list[3], (L, HV * DV), 1.0, 6.0, ((0, 256),)),
        "write_strength": draw_write_strength(jax.random.fold_in(key_list[11], 71), 0),
        "log_decay": draw_log_decay(jax.random.fold_in(key_list[11], 71), 0),
        "filter_query": normal_values(key_list[6], (KW, HK * DK), 0.5, 3.0, ((1, 8),)),
        "filter_key": normal_values(key_list[7], (KW, HK * DK), 0.5, 3.0, ((1, 8),)),
        "filter_value": normal_values(key_list[8], (KW, HV * DV), 0.5, 3.0, ((1, 8),)),
        "norm_gain": jnp.clip(1.0 + 0.18 * jax.random.normal(key_list[9], (DV,), jnp.float32), 0.1, 1.9),
        "out_weight": normal_values(key_list[10], (HV * DV, D), (HV * DV) ** -0.5, 0.09375, ((0, 8),)),
    }


exact_mode = lax.Precision.HIGHEST
norm_floor = 1e-06

def stretch_terms(query_rows, unit_keys, values, strength, forgetting_rates):
    block_width = forgetting_rates.shape[-1]
    value_width = values.shape[-1]
    key_width = unit_keys.shape[-1]
    token_index = lax.broadcasted_iota(jnp.int32, (block_width, block_width), 0)
    column_index = lax.broadcasted_iota(jnp.int32, (block_width, block_width), 1)
    inclusive = (column_index <= token_index).astype(jnp.float32)
    strict = (column_index < token_index).astype(jnp.float32)
    cumulative = jnp.cumsum(forgetting_rates, axis=-1)
    spread = cumulative[..., :, None] - cumulative[..., None, :]
    ratios = jnp.exp(spread * inclusive) * inclusive
    key_key = jnp.einsum('...id,...jd->...ij', unit_keys, unit_keys, precision=exact_mode)
    query_key = jnp.einsum('...id,...jd->...ij', query_rows, unit_keys, precision=exact_mode)
    lower_part = strength[..., :, None] * key_key * ratios * strict
    query_mix = query_key * ratios
    growth = jnp.exp(cumulative)
    right_side = jnp.concatenate([strength[..., None] * values, (strength * growth)[..., None] * unit_keys], axis=-1)
    system = lower_part + jnp.eye(block_width, dtype=jnp.float32)
    solved = jax.scipy.linalg.solve_triangular(system, right_side, lower=True, unit_diagonal=True)
    written = solved[..., :value_width]
    erased = solved[..., value_width:]
    tail_decay = jnp.exp(cumulative[..., -1:] - cumulative)
    tailed = unit_keys * tail_decay[..., None]
    carry_map = jnp.exp(cumulative[..., -1])[..., None, None] * jnp.eye(key_width, dtype=jnp.float32) - jnp.einsum('...id,...ie->...de', tailed, erased, precision=exact_mode)
    carry_add = jnp.einsum('...id,...ie->...de', tailed, written, precision=exact_mode)
    local_out = jnp.einsum('...ij,...je->...ie', query_mix, written, precision=exact_mode)
    entry_map = growth[..., None] * query_rows - jnp.einsum('...ij,...jd->...id', query_mix, erased, precision=exact_mode)
    return (carry_map, carry_add, local_out, entry_map)

def causal_filter(signal, filter_taps):
    kernel_width = filter_taps.shape[0]
    length = signal.shape[0]
    padded = jnp.concatenate([jnp.zeros((kernel_width - 1, signal.shape[1]), jnp.float32), signal.astype(jnp.float32)], axis=0)
    summed = jnp.zeros(signal.shape, jnp.float32)
    for offset in range(kernel_width):
        summed = summed + filter_taps[offset].astype(jnp.float32) * padded[offset:offset + length]
    return jax.nn.silu(summed)

def unit_rows(field):
    return field / jnp.sqrt(lax.optimization_barrier(jnp.sum(field * field, axis=-1, keepdims=True)) + norm_floor)

def reference(query_input, key_input, value_input, gate_input, write_strength, log_decay, filter_query, filter_key, filter_value, norm_gain, out_weight):
    query_rows = unit_rows(causal_filter(query_input, filter_query).reshape(L, HK, DK)) * DK ** (-0.5)
    unit_keys = unit_rows(causal_filter(key_input, filter_key).reshape(L, HK, DK))
    values = causal_filter(value_input, filter_value).reshape(L, HV, DV)
    sharing = HV // HK
    blocks = L // CH

    def one_head(head_index):
        source = head_index // sharing
        head_query = lax.dynamic_index_in_dim(query_rows, source, 1, keepdims=False).reshape(blocks, CH, DK)
        head_key = lax.dynamic_index_in_dim(unit_keys, source, 1, keepdims=False).reshape(blocks, CH, DK)
        head_value = lax.dynamic_index_in_dim(values, head_index, 1, keepdims=False).reshape(blocks, CH, DV)
        strength = lax.dynamic_index_in_dim(write_strength, head_index, 1, keepdims=False).astype(jnp.float32).reshape(blocks, CH)
        forgetting_rates = lax.dynamic_index_in_dim(log_decay, head_index, 1, keepdims=False).astype(jnp.float32).reshape(blocks, CH)
        carry_map, carry_add, local_out, entry_map = stretch_terms(head_query, head_key, head_value, strength, forgetting_rates)

        def advance(running, pieces):
            block_map, block_add, block_out, block_entry = pieces
            emitted = block_out + jnp.dot(block_entry, running, precision=exact_mode)
            return (jnp.dot(block_map, running, precision=exact_mode) + block_add, emitted)
        final_state, outputs = lax.scan(advance, jnp.zeros((DK, DV), jnp.float32), (carry_map, carry_add, local_out, entry_map))
        return outputs.reshape(L, DV)
    core_out = lax.map(one_head, jnp.arange(HV, dtype=jnp.int32))
    core_out = jnp.transpose(core_out, (1, 0, 2))
    inverse_rms = lax.rsqrt(lax.optimization_barrier(jnp.mean(core_out * core_out, axis=-1, keepdims=True)) + norm_floor)
    gating = jax.nn.silu(gate_input.astype(jnp.float32)).reshape(L, HV, DV)
    normed = (core_out * inverse_rms * norm_gain * gating).astype(jnp.bfloat16).reshape(L, HV * DV)
    return jnp.dot(normed.astype(jnp.float32), out_weight.astype(jnp.float32), preferred_element_type=jnp.float32).astype(jnp.bfloat16)
```

```python
import functools

import jax
import jax.numpy as jnp
from jax import lax
from jax.experimental import pallas as pl
from jax.experimental.pallas import tpu as pltpu
from jax.sharding import PartitionSpec as P

HK = 16
HV = 32
DK = 128
DV = 128
CH = 64
PAD = 16
NZ = 8
ROWS = 64
norm_floor = 1e-06
F32 = jnp.float32
BF16 = jnp.bfloat16
MESH = pl.DeviceIdType.MESH
VMEM_LIMIT = 60 * 1024 * 1024


def halves(x):
    high = x.astype(BF16)
    low = (x - high.astype(F32)).astype(BF16)
    return high, low


def dot(a, b, dims=((1,), (0,))):
    return lax.dot_general(a, b, (dims, ((), ())), preferred_element_type=F32)


def dot3(a, b, dims=((1,), (0,))):
    ah, al = a
    bh, bl = b
    return dot(ah, bh, dims) + (dot(ah, bl, dims) + dot(al, bh, dims))


def exchange_kernel(
    ns, nh, q, k, v, g, ws, ld, qo, ko, vo, go, wo, lo, send_sem, recv_sem, halo_send, halo_recv, own_sem
):
    seq = lax.axis_index("seq")
    me = lax.axis_index("head")
    rows = q.shape[0]
    ins = (q, k, v, g, ws, ld)
    outs = (qo, ko, vo, go, wo, lo)
    pads = (PAD, PAD, PAD, 0, 0, 0)
    last = jnp.logical_and(me == nh - 1, seq < ns - 1)
    barrier = pltpu.get_barrier_semaphore()
    for d in range(1, nh):
        pl.semaphore_signal(
            barrier, inc=1, device_id=(seq, lax.rem(me + d, nh)), device_id_type=MESH
        )

    @pl.when(seq > 0)
    def _():
        pl.semaphore_signal(barrier, inc=1, device_id=(seq - 1, nh - 1), device_id_type=MESH)

    @pl.when(last)
    def _():
        for d in range(nh):
            pl.semaphore_signal(barrier, inc=1, device_id=(seq + 1, d), device_id_type=MESH)

    def piece(ref, out, who):
        if out.shape[1] == ref.shape[1]:
            return ref
        width = out.shape[1]
        return ref.at[:, pl.ds(pl.multiple_of(who * width, width), width)]

    def own(a):
        return pltpu.make_async_copy(
            piece(ins[a], outs[a], me),
            outs[a].at[pl.ds(pl.multiple_of(pads[a] + me * rows, 16), rows), :],
            own_sem.at[a],
        )

    for a in range(6):
        own(a).start()
    pl.semaphore_wait(
        barrier, nh - 1 + jnp.where(seq > 0, 1, 0) + jnp.where(last, nh, 0)
    )

    def across(d, a, to, source):
        return pltpu.make_async_remote_copy(
            src_ref=piece(ins[a], outs[a], to),
            dst_ref=outs[a].at[pl.ds(pl.multiple_of(pads[a] + source * rows, 16), rows), :],
            send_sem=send_sem.at[d - 1, a],
            recv_sem=recv_sem.at[d - 1, a],
            device_id=(seq, to),
            device_id_type=MESH,
        )

    def halo(d, a):
        width = outs[a].shape[1]
        return pltpu.make_async_remote_copy(
            src_ref=ins[a].at[pl.ds(rows - PAD, PAD), pl.ds(d * width, width)],
            dst_ref=outs[a].at[pl.ds(0, PAD), :],
            send_sem=halo_send.at[d, a],
            recv_sem=halo_recv.at[a],
            device_id=(seq + 1, d),
            device_id_type=MESH,
        )

    order = [d for d in (4, 3, 5, 2, 6, 1, 7) if d < nh]
    for d in order:
        for a in range(6):
            across(d, a, lax.rem(me + d, nh), me).start()

    @pl.when(last)
    def _():
        for d in range(nh):
            for a in range(3):
                halo(d, a).start()

    for d in order:
        for a in range(6):
            across(d, a, lax.rem(me + d, nh), lax.rem(me + nh - d, nh)).wait()

    @pl.when(seq > 0)
    def _():
        for a in range(3):
            halo(0, a).wait_recv()

    @pl.when(last)
    def _():
        for d in range(nh):
            for a in range(3):
                halo(d, a).wait_send()

    for a in range(6):
        own(a).wait()


def exchange(ns, nh, arrays):
    rows = arrays[0].shape[0]
    total = rows * nh
    shapes = []
    for i, x in enumerate(arrays):
        width = x.shape[1] // nh if i < 4 else x.shape[1]
        shapes.append(jax.ShapeDtypeStruct((total + (PAD if i < 3 else 0), width), x.dtype))
    return pl.pallas_call(
        functools.partial(exchange_kernel, ns, nh),
        name="token_exchange",
        out_shape=shapes,
        in_specs=[pl.BlockSpec(memory_space=pl.ANY)] * 6,
        out_specs=[pl.BlockSpec(memory_space=pltpu.VMEM)] * 6,
        scratch_shapes=[
            pltpu.SemaphoreType.DMA((nh - 1, 6)),
            pltpu.SemaphoreType.DMA((nh - 1, 6)),
            pltpu.SemaphoreType.DMA((nh, 3)),
            pltpu.SemaphoreType.DMA((3,)),
            pltpu.SemaphoreType.DMA((6,)),
        ],
        compiler_params=pltpu.CompilerParams(
            collective_id=0, has_side_effects=True, vmem_limit_bytes=VMEM_LIMIT
        ),
    )(*arrays)


def local_kernel(
    where_ref, q_ref, k_ref, v_ref, ws_ref, ld_ref, fq_ref, fk_ref, fv_ref,
    chain_ref, qeff_ref, olocal_ref,
    key_s, query_s, w_s, e_s, mix_s, grow_s, tail_s, gamma_s, state_s,
):
    seq = where_ref[0]
    head = where_ref[1]
    tokens = ws_ref.shape[0]
    blocks = tokens // CH
    nheads = v_ref.shape[1] // DV
    nkeys = k_ref.shape[1] // DK
    share = nheads // nkeys
    row = lax.broadcasted_iota(jnp.int32, (CH, CH), 0)
    col = lax.broadcasted_iota(jnp.int32, (CH, CH), 1)
    incl = col <= row
    strict = col < row
    eye = (col == row).astype(F32)
    lower_ones = incl.astype(F32).astype(BF16)
    upper_ones = (row <= col).astype(F32).astype(BF16)
    allh = ws_ref.shape[1]
    pick = (
        lax.broadcasted_iota(jnp.int32, (allh, 128), 0)
        == head * nheads + lax.broadcasted_iota(jnp.int32, (allh, 128), 1)
    )
    pick = jnp.logical_and(pick, lax.broadcasted_iota(jnp.int32, (allh, 128), 1) < nheads)
    pick = pick.astype(F32).astype(BF16)
    pick_t = (
        lax.broadcasted_iota(jnp.int32, (8, allh), 1)
        == head * nheads + lax.broadcasted_iota(jnp.int32, (8, allh), 0)
    )
    pick_t = jnp.logical_and(pick_t, lax.broadcasted_iota(jnp.int32, (8, allh), 0) < nheads)
    pick_t = pick_t.astype(F32).astype(BF16)
    masks = []
    size = 1
    while size < CH:
        masks.append(
            jnp.logical_and(
                jnp.logical_and((row // size) % 2 == 1, (col // size) + 1 == row // size), strict
            )
        )
        size *= 2

    def filtered(ref, taps, start, lo, width):
        x = ref[pl.ds(start, CH + PAD), lo : lo + width].astype(F32)
        edge = lax.broadcasted_iota(jnp.int32, (CH + PAD, width), 0) < PAD
        x = jnp.where(jnp.logical_and(edge, jnp.logical_and(seq == 0, start == 0)), 0.0, x)
        total = None
        for j in range(4):
            term = taps[j : j + 1, lo : lo + width].astype(F32) * x[PAD - 3 + j : PAD - 3 + j + CH]
            total = term if total is None else total + term
        return total / (1.0 + jnp.exp(-total))

    def block_terms(c):
        start = pl.multiple_of(c * CH, CH)
        rows = pl.ds(start, CH)
        wsc = ws_ref[rows, :]
        ldc = ld_ref[rows, :]
        beta_c = dot(wsc, pick)
        dec_c = dot(ldc, pick)
        beta_r = dot(pick_t, wsc, ((1,), (1,)))
        dec_r = dot(pick_t, ldc, ((1,), (1,)))
        cum_c = dot(lower_ones, dec_c.astype(BF16))
        cum_r = dot(dec_r.astype(BF16), upper_ones)
        grow_c = jnp.exp(cum_c)
        grow_r = jnp.exp(cum_r)
        tail_c = jnp.exp(cum_c[CH - 1 : CH, :] - cum_c)
        gamma = grow_c[CH - 1 : CH, :]
        gamma_s[pl.ds(pl.multiple_of(c * 8, 8), 8), :] = jnp.broadcast_to(gamma, (8, 128))
        grow_s[rows, :] = grow_c
        tail_s[rows, :] = tail_c
        for p in range(nkeys):
            lanes = slice(p * DK, (p + 1) * DK)
            key = filtered(k_ref, fk_ref, start, p * DK, DK)
            key = key * lax.rsqrt(jnp.sum(key * key, axis=1, keepdims=True) + norm_floor)
            query = filtered(q_ref, fq_ref, start, p * DK, DK)
            query = query * (
                lax.rsqrt(jnp.sum(query * query, axis=1, keepdims=True) + norm_floor) * DK ** (-0.5)
            )
            key_s[rows, lanes] = key
            query_s[rows, lanes] = query
            kh, kl = halves(key)
            qh, ql = halves(query)
            kk = dot3((kh, kl), (kh, kl), ((1,), (1,)))
            qk = dot3((qh, ql), (kh, kl), ((1,), (1,)))
            for s in range(share):
                h = p * share + s
                spread = cum_c[:, h : h + 1] - cum_r[h : h + 1, :]
                ratios = jnp.where(incl, jnp.exp(jnp.where(incl, spread, 0.0)), 0.0)
                lower = jnp.where(strict, beta_c[:, h : h + 1] * kk * ratios, 0.0)
                mix_s[h, rows, :] = qk * ratios
                inv = eye - jnp.where(masks[0], lower, 0.0)
                for m in masks[1:]:
                    iv = halves(inv)
                    t = dot3(halves(jnp.where(m, lower, 0.0)), iv)
                    inv = inv - dot3(iv, halves(t))
                vals = filtered(v_ref, fv_ref, start, h * DV, DV)
                w_s[rows, h * DV : (h + 1) * DV] = dot3(
                    halves(inv * beta_r[h : h + 1, :]), halves(vals)
                )
                e_s[rows, h * DK : (h + 1) * DK] = dot3(
                    halves(inv * (beta_r[h : h + 1, :] * grow_r[h : h + 1, :])), (kh, kl)
                )

    def first(i, carry):
        block_terms(i)
        return carry

    lax.fori_loop(0, blocks, first, 0)

    eye_k = (
        lax.broadcasted_iota(jnp.int32, (DK, DK + DV), 0)
        == lax.broadcasted_iota(jnp.int32, (DK, DK + DV), 1)
    ).astype(F32)
    for h in range(nheads):
        state_s[h] = eye_k

    def second(c, carry):
        start = pl.multiple_of(c * CH, CH)
        rows = pl.ds(start, CH)
        grow_c = grow_s[rows, :]
        tail_c = tail_s[rows, :]
        gamma = gamma_s[pl.ds(pl.multiple_of(c * 8, 8), 8), :]
        for h in range(nheads):
            p = h // share
            key = key_s[rows, p * DK : (p + 1) * DK]
            query = query_s[rows, p * DK : (p + 1) * DK]
            state = state_s[h]
            e = e_s[rows, h * DK : (h + 1) * DK]
            w = w_s[rows, h * DV : (h + 1) * DV]
            left = jnp.concatenate([e, query * grow_c[:, h : h + 1]], axis=0)
            x = dot3(halves(left), halves(state))
            fresh = jnp.concatenate([-x[:CH, :DK], w - x[:CH, DK:]], axis=1)
            fr = halves(fresh)
            y = x[CH:] + dot3(halves(mix_s[h, rows, :]), fr)
            tailed = key * tail_c[:, h : h + 1]
            state_s[h] = gamma[0:1, h : h + 1] * state + dot3(
                halves(tailed), fr, ((0,), (0,))
            )
            qeff_ref[rows, h * DK : (h + 1) * DK] = y[:, :DK]
            olocal_ref[rows, h * DV : (h + 1) * DV] = y[:, DK:]
        return carry

    lax.fori_loop(0, blocks, second, 0)
    for h in range(nheads):
        for part in range(2):
            t = state_s[h, :, part * DK : (part + 1) * DK].T
            for r in range(DK // ROWS):
                chain_ref[h * 2 * (DK // ROWS) + part * (DK // ROWS) + r] = t[
                    r * ROWS : (r + 1) * ROWS
                ]


def local_terms(where, q, k, v, ws, ld, fq, fk, fv):
    tokens = ws.shape[0]
    nheads = v.shape[1] // DV
    nkeys = k.shape[1] // DK
    vm = pl.BlockSpec(memory_space=pltpu.VMEM)
    return pl.pallas_call(
        local_kernel,
        name="local_terms",
        out_shape=[
            jax.ShapeDtypeStruct((nheads * 2 * DK // ROWS, ROWS, DK), F32),
            jax.ShapeDtypeStruct((tokens, nheads * DK), F32),
            jax.ShapeDtypeStruct((tokens, nheads * DV), F32),
        ],
        in_specs=[pl.BlockSpec(memory_space=pltpu.SMEM)] + [vm] * 8,
        out_specs=[vm] * 3,
        scratch_shapes=[
            pltpu.VMEM((tokens, nkeys * DK), F32),
            pltpu.VMEM((tokens, nkeys * DK), F32),
            pltpu.VMEM((tokens, nheads * DV), F32),
            pltpu.VMEM((tokens, nheads * DK), F32),
            pltpu.VMEM((nheads, tokens, CH), F32),
            pltpu.VMEM((tokens, 128), F32),
            pltpu.VMEM((tokens, 128), F32),
            pltpu.VMEM((tokens // CH * 8, 128), F32),
            pltpu.VMEM((nheads, DK, DK + DV), F32),
        ],
        compiler_params=pltpu.CompilerParams(vmem_limit_bytes=VMEM_LIMIT),
    )(where, q, k, v, ws, ld, fq, fk, fv)


def chain_kernel(
    ns, nz, own_ref, entry_ref, before, here, map_h, map_l, earlier, later,
    pre_send, pre_recv, far_send, far_recv, relay_send, relay_two,
):
    seq = lax.axis_index("seq")
    head = lax.axis_index("head")
    ny = ns // nz
    z = lax.rem(seq, nz)
    y = seq // nz
    pieces = own_ref.shape[0]
    per_head = 2 * DK // ROWS
    half = per_head // 2
    nheads = pieces // per_head
    base = y * nz
    up = base + lax.rem(z + 1, nz)
    down = base + lax.rem(z + nz - 1, nz)
    mid = nz // 2
    is_end = z == nz - 1

    barrier = pltpu.get_barrier_semaphore()
    for other in (up, down):
        pl.semaphore_signal(barrier, inc=1, device_id=(other, head), device_id_type=MESH)

    @pl.when(jnp.logical_and(is_end, y > 0))
    def _():
        pl.semaphore_signal(barrier, inc=1, device_id=(seq - nz, head), device_id_type=MESH)

    @pl.when(jnp.logical_and(is_end, y < ny - 1))
    def _():
        pl.semaphore_signal(barrier, inc=1, device_id=(seq + nz, head), device_id_type=MESH)

    def split_maps(ref):
        for h in range(nheads):
            for r in range(half):
                hi, lo = halves(ref[h * per_head + r])
                map_h[h, r * ROWS : (r + 1) * ROWS, :] = hi
                map_l[h, r * ROWS : (r + 1) * ROWS, :] = lo

    split_maps(own_ref)
    pl.semaphore_wait(
        barrier,
        2
        + jnp.where(jnp.logical_and(is_end, y > 0), 1, 0)
        + jnp.where(jnp.logical_and(is_end, y < ny - 1), 1, 0),
    )

    def onward(n, source):
        return pltpu.make_async_remote_copy(
            src_ref=source.at[n],
            dst_ref=before.at[n],
            send_sem=pre_send.at[n],
            recv_sem=pre_recv.at[n],
            device_id=(up, head),
            device_id_type=MESH,
        )

    def to_group(m, source):
        return pltpu.make_async_remote_copy(
            src_ref=source.at[m],
            dst_ref=earlier.at[m],
            send_sem=far_send.at[m],
            recv_sem=far_recv.at[m],
            device_id=(seq + nz, head),
            device_id_type=MESH,
        )

    def relay(m, to, sem):
        return pltpu.make_async_remote_copy(
            src_ref=earlier.at[m],
            dst_ref=earlier.at[m],
            send_sem=sem.at[m],
            recv_sem=far_recv.at[m],
            device_id=(to, head),
            device_id_type=MESH,
        )

    def times_map(x, h):
        return dot3(halves(x), (map_h[h], map_l[h]))

    @pl.when(z == 0)
    def _():
        def send(n, c):
            onward(n, own_ref).start()
            return c

        lax.fori_loop(0, pieces, send, 0)

    @pl.when(z > 0)
    def _():
        def step(n, c):
            onward(n, here).wait_recv()
            h = n // per_head
            part = lax.rem(n, per_head)
            r = times_map(before[n], h)
            here[n] = r + jnp.where(part >= half, own_ref[n], 0.0)

            @pl.when(z < nz - 1)
            def _():
                onward(n, here).start()

            return c

        lax.fori_loop(0, pieces, step, 0)

    npe = nheads * half

    @pl.when(is_end)
    def _():
        @pl.when(y == 0)
        def _():
            def send(m, c):
                h = m // half
                r = lax.rem(m, half)
                later[m] = here[h * per_head + half + r]
                to_group(m, later).start()
                return c

            lax.fori_loop(0, npe, send, 0)

        @pl.when(y > 0)
        def _():
            split_maps(here)

            def step(m, c):
                to_group(m, later).wait_recv()
                relay(m, down, relay_send).start()
                relay(m, up, relay_two).start()

                @pl.when(y < ny - 1)
                def _():
                    h = m // half
                    r = lax.rem(m, half)
                    later[m] = times_map(earlier[m], h) + here[h * per_head + half + r]
                    to_group(m, later).start()

                return c

            lax.fori_loop(0, npe, step, 0)

    @pl.when(jnp.logical_and(jnp.logical_not(is_end), y > 0))
    def _():
        def step(m, c):
            relay(m, down, relay_send).wait_recv()

            @pl.when(z > mid)
            def _():
                relay(m, down, relay_send).start()

            @pl.when(z < mid - 1)
            def _():
                relay(m, up, relay_two).start()

            return c

        lax.fori_loop(0, npe, step, 0)

    @pl.when(z == 0)
    def _():
        for m in range(npe):
            entry_ref[m] = jnp.where(y > 0, earlier[m], 0.0)

    @pl.when(z > 0)
    def _():
        @pl.when(y == 0)
        def _():
            for m in range(npe):
                entry_ref[m] = before[(m // half) * per_head + half + m % half]

        @pl.when(y > 0)
        def _():
            split_maps(before)
            for m in range(npe):
                entry_ref[m] = (
                    times_map(earlier[m], m // half)
                    + before[(m // half) * per_head + half + m % half]
                )

    @pl.when(z < nz - 1)
    def _():
        def done(n, c):
            onward(n, own_ref).wait_send()
            return c

        lax.fori_loop(0, pieces, done, 0)

    @pl.when(jnp.logical_and(is_end, y < ny - 1))
    def _():
        def done(m, c):
            to_group(m, later).wait_send()
            return c

        lax.fori_loop(0, npe, done, 0)

    @pl.when(jnp.logical_and(y > 0, z > mid))
    def _():
        def done(m, c):
            relay(m, down, relay_send).wait_send()
            return c

        lax.fori_loop(0, npe, done, 0)

    @pl.when(jnp.logical_and(y > 0, jnp.logical_or(is_end, z < mid - 1)))
    def _():
        def done(m, c):
            relay(m, up, relay_two).wait_send()
            return c

        lax.fori_loop(0, npe, done, 0)


def state_chain(ns, nz, own):
    pieces = own.shape[0]
    nheads = pieces * ROWS // (2 * DK)
    npe = pieces // 2
    vm = pl.BlockSpec(memory_space=pltpu.VMEM)
    return pl.pallas_call(
        functools.partial(chain_kernel, ns, nz),
        name="state_chain",
        out_shape=jax.ShapeDtypeStruct((npe, ROWS, DK), F32),
        in_specs=[vm],
        out_specs=vm,
        scratch_shapes=[
            pltpu.VMEM((pieces, ROWS, DK), F32),
            pltpu.VMEM((pieces, ROWS, DK), F32),
            pltpu.VMEM((nheads, DK, DK), BF16),
            pltpu.VMEM((nheads, DK, DK), BF16),
            pltpu.VMEM((npe, ROWS, DK), F32),
            pltpu.VMEM((npe, ROWS, DK), F32),
            pltpu.SemaphoreType.DMA((pieces,)),
            pltpu.SemaphoreType.DMA((pieces,)),
            pltpu.SemaphoreType.DMA((npe,)),
            pltpu.SemaphoreType.DMA((npe,)),
            pltpu.SemaphoreType.DMA((npe,)),
            pltpu.SemaphoreType.DMA((npe,)),
        ],
        compiler_params=pltpu.CompilerParams(
            collective_id=1, has_side_effects=True, vmem_limit_bytes=VMEM_LIMIT
        ),
    )(own)


def output_kernel(qeff_ref, olocal_ref, entry_ref, gate_ref, gain_ref, weight_ref, part_ref, normed_s):
    nheads = qeff_ref.shape[1] // DK
    tokens = qeff_ref.shape[0]
    pieces = DV // ROWS
    step_rows = 128
    for h in range(nheads):
        entry = jnp.concatenate([entry_ref[h * pieces + r] for r in range(pieces)], axis=0)
        entry = halves(entry)
        lanes = slice(h * DV, (h + 1) * DV)

        def step(i, c):
            rows = pl.ds(pl.multiple_of(i * step_rows, step_rows), step_rows)
            core = olocal_ref[rows, lanes] + dot3(
                halves(qeff_ref[rows, lanes]), entry, ((1,), (1,))
            )
            scale = lax.rsqrt(jnp.mean(core * core, axis=1, keepdims=True) + norm_floor)
            gate = gate_ref[rows, lanes].astype(F32)
            gate = gate / (1.0 + jnp.exp(-gate))
            normed_s[rows, lanes] = (core * scale * gain_ref[...] * gate).astype(BF16)
            return c

        lax.fori_loop(0, tokens // step_rows, step, 0)

    wide = 256

    def project(i, c):
        rows = pl.ds(pl.multiple_of(i * wide, wide), wide)
        for j in range(weight_ref.shape[1] // wide):
            part_ref[rows, j * wide : (j + 1) * wide] = dot(
                normed_s[rows, :], weight_ref[:, j * wide : (j + 1) * wide]
            ).astype(BF16)
        return c

    lax.fori_loop(0, tokens // wide, project, 0)


def output_part(qeff, olocal, entry, gate, gain, weight):
    vm = pl.BlockSpec(memory_space=pltpu.VMEM)
    return pl.pallas_call(
        output_kernel,
        name="gated_projection",
        out_shape=jax.ShapeDtypeStruct((qeff.shape[0], weight.shape[1]), BF16),
        in_specs=[vm] * 6,
        out_specs=vm,
        scratch_shapes=[pltpu.VMEM((qeff.shape[0], weight.shape[0]), BF16)],
        compiler_params=pltpu.CompilerParams(vmem_limit_bytes=VMEM_LIMIT),
    )(qeff, olocal, entry, gate, gain, weight)


def sum_kernel(nh, part_ref, out_ref, twin, mine, landed, twin_send, twin_recv, send_sem, recv_sem):
    seq = lax.axis_index("seq")
    me = lax.axis_index("head")
    chips = nh // 2
    chip = me // 2
    core = lax.rem(me, 2)
    other = 1 - core
    rows = out_ref.shape[0]
    barrier = pltpu.get_barrier_semaphore()
    pl.semaphore_signal(barrier, inc=1, device_id=(seq, chip * 2 + other), device_id_type=MESH)
    for d in range(1, chips):
        pl.semaphore_signal(
            barrier, inc=1, device_id=(seq, lax.rem(chip + d, chips) * 2 + core), device_id_type=MESH
        )
    pl.semaphore_wait(barrier, chips)

    def block(d, side):
        start = (lax.rem(chip + d, chips) * 2 + side) * rows
        return pl.ds(pl.multiple_of(start, 64), rows)

    def to_twin(d):
        return pltpu.make_async_remote_copy(
            src_ref=part_ref.at[block(d, other), :],
            dst_ref=twin.at[d],
            send_sem=twin_send.at[d],
            recv_sem=twin_recv.at[d],
            device_id=(seq, chip * 2 + other),
            device_id_type=MESH,
        )

    def away(d):
        return pltpu.make_async_remote_copy(
            src_ref=mine.at[d],
            dst_ref=landed.at[d],
            send_sem=send_sem.at[d],
            recv_sem=recv_sem.at[d],
            device_id=(seq, lax.rem(chip + d, chips) * 2 + core),
            device_id_type=MESH,
        )

    order = [d for d in (2, 1, 3, 0) if d < chips]
    for d in order:
        to_twin(d).start()
    total = None
    for d in order:
        to_twin(d).wait_recv()
        both = part_ref[block(d, core), :].astype(F32) + twin[d].astype(F32)
        if d:
            mine[d] = both.astype(BF16)
            away(d).start()
        else:
            total = both
    for d in order:
        if d:
            away(d).wait_recv()
            total = total + landed[d].astype(F32)
    out_ref[...] = total.astype(BF16)
    for d in order:
        to_twin(d).wait_send()
        if d:
            away(d).wait_send()


def row_sums(nh, part):
    rows = part.shape[0] // nh
    width = part.shape[1]
    chips = nh // 2
    vm = pl.BlockSpec(memory_space=pltpu.VMEM)
    return pl.pallas_call(
        functools.partial(sum_kernel, nh),
        name="row_sums",
        out_shape=jax.ShapeDtypeStruct((rows, width), BF16),
        in_specs=[vm],
        out_specs=vm,
        scratch_shapes=[
            pltpu.VMEM((chips, rows, width), BF16),
            pltpu.VMEM((chips, rows, width), BF16),
            pltpu.VMEM((chips, rows, width), BF16),
            pltpu.SemaphoreType.DMA((chips,)),
            pltpu.SemaphoreType.DMA((chips,)),
            pltpu.SemaphoreType.DMA((chips,)),
            pltpu.SemaphoreType.DMA((chips,)),
        ],
        compiler_params=pltpu.CompilerParams(
            collective_id=2, has_side_effects=True, vmem_limit_bytes=VMEM_LIMIT
        ),
    )(part)


def on_device(
    ns, nh, query_input, key_input, value_input, gate_input, write_strength, log_decay,
    filter_query, filter_key, filter_value, norm_gain, out_weight,
):
    q, k, v, gate, ws, ld = exchange(
        ns, nh, (query_input, key_input, value_input, gate_input, write_strength, log_decay)
    )
    where = jnp.stack([lax.axis_index("seq"), lax.axis_index("head")]).astype(jnp.int32)
    own, qeff, olocal = local_terms(where, q, k, v, ws, ld, filter_query, filter_key, filter_value)
    entry = state_chain(ns, NZ, own)
    part = output_part(qeff, olocal, entry, gate, norm_gain.reshape(1, DV), out_weight)
    return row_sums(nh, part)


def solution(mesh):
    placed = (
        P(("seq", "head"), None),
        P(("seq", "head"), None),
        P(("seq", "head"), None),
        P(("seq", "head"), None),
        P(("seq", "head"), None),
        P(("seq", "head"), None),
        P(None, "head"),
        P(None, "head"),
        P(None, "head"),
        P(),
        P("head", None),
    )
    return jax.shard_map(
        functools.partial(on_device, mesh.shape["seq"], mesh.shape["head"]),
        mesh=mesh,
        in_specs=placed,
        out_specs=P(("seq", "head"), None),
        check_vma=False,
    )
```

```python
import functools

import jax
import jax.numpy as jnp
from jax import lax
from jax.experimental import pallas as pl
from jax.experimental.pallas import tpu as pltpu
from jax.sharding import PartitionSpec as P

HK = 16
HV = 32
DK = 128
DV = 128
CH = 64
PAD = 16
NZ = 8
ROWS = 64
norm_floor = 1e-06
F32 = jnp.float32
BF16 = jnp.bfloat16
MESH = pl.DeviceIdType.MESH
VMEM_LIMIT = 60 * 1024 * 1024


def halves(x):
    high = x.astype(BF16)
    low = (x - high.astype(F32)).astype(BF16)
    return high, low


def dot(a, b, dims=((1,), (0,))):
    return lax.dot_general(a, b, (dims, ((), ())), preferred_element_type=F32)


def dot3(a, b, dims=((1,), (0,))):
    ah, al = a
    bh, bl = b
    return dot(ah, bh, dims) + (dot(ah, bl, dims) + dot(al, bh, dims))


def exchange_kernel(
    ns, nh, via, q, k, v, wl, qo, ko, vo, wlo, rq, rk, rv,
    send_sem, recv_sem, hop_send, hop_recv, pass_send, pass_recv, halo_send, halo_recv, own_sem,
):
    seq = lax.axis_index("seq")
    me = lax.axis_index("head")
    rows = q.shape[0]
    chips = nh // 2
    chip = me // 2
    odd = lax.rem(me, 2) == 1
    ins = (q, k, v, wl)
    outs = (qo, ko, vo, wlo)
    pads = (PAD, PAD, PAD, 0)
    hops = (rq, rk, rv)
    nbr = lax.rem(chip + via, chips) * 2 + 1
    far = lax.rem(chip + 2, chips)
    next_far = lax.rem(chip + via, chips)
    origin = lax.rem(chip + chips - via, chips) * 2 + 1
    last = jnp.logical_and(me == nh - 1, seq < ns - 1)
    barrier = pltpu.get_barrier_semaphore()
    for d in range(1, nh):
        pl.semaphore_signal(
            barrier, inc=1, device_id=(seq, lax.rem(me + d, nh)), device_id_type=MESH
        )

    @pl.when(seq > 0)
    def _():
        pl.semaphore_signal(barrier, inc=1, device_id=(seq - 1, nh - 1), device_id_type=MESH)

    @pl.when(last)
    def _():
        for d in range(nh):
            pl.semaphore_signal(barrier, inc=1, device_id=(seq + 1, d), device_id_type=MESH)

    def piece(a, who):
        if a == 3:
            return ins[a]
        width = outs[a].shape[1]
        return ins[a].at[:, pl.ds(pl.multiple_of(who * width, width), width)]

    def place(a, who):
        return outs[a].at[pl.ds(pl.multiple_of(pads[a] + who * rows, 16), rows), :]

    def own(a):
        return pltpu.make_async_copy(piece(a, me), place(a, me), own_sem.at[a])

    for a in range(4):
        own(a).start()
    pl.semaphore_wait(barrier, nh - 1 + jnp.where(seq > 0, 1, 0) + jnp.where(last, nh, 0))

    def across(d, a, to, source):
        return pltpu.make_async_remote_copy(
            src_ref=piece(a, to),
            dst_ref=place(a, source),
            send_sem=send_sem.at[d - 1, a],
            recv_sem=recv_sem.at[d - 1, a],
            device_id=(seq, to),
            device_id_type=MESH,
        )

    def halo(d, a):
        width = outs[a].shape[1]
        return pltpu.make_async_remote_copy(
            src_ref=ins[a].at[pl.ds(rows - PAD, PAD), pl.ds(d * width, width)],
            dst_ref=outs[a].at[pl.ds(0, PAD), :],
            send_sem=halo_send.at[d, a],
            recv_sem=halo_recv.at[a],
            device_id=(seq + 1, d),
            device_id_type=MESH,
        )

    def hop(side, a):
        return pltpu.make_async_remote_copy(
            src_ref=piece(a, far * 2 + side),
            dst_ref=hops[a].at[side],
            send_sem=hop_send.at[side, a],
            recv_sem=hop_recv.at[side, a],
            device_id=(seq, nbr),
            device_id_type=MESH,
        )

    def passed(side, a):
        return pltpu.make_async_remote_copy(
            src_ref=hops[a].at[side],
            dst_ref=place(a, origin),
            send_sem=pass_send.at[side, a],
            recv_sem=pass_recv.at[a],
            device_id=(seq, next_far * 2 + side),
            device_id_type=MESH,
        )

    @pl.when(last)
    def _():
        for d in range(nh):
            for a in range(3):
                halo(d, a).start()

    def target(d):
        return lax.rem(me + d, nh)

    def source(d):
        return lax.rem(me + nh - d, nh)

    @pl.when(odd)
    def _():
        for a in range(3):
            for side in range(2):
                hop(side, a).start()
        for d in (3, 4):
            across(d, 3, target(d), me).start()
        for a in (3, 0, 1, 2):
            for d in (2, 6, 5, 1, 7):
                across(d, a, target(d), me).start()

    @pl.when(jnp.logical_not(odd))
    def _():
        for a in (3, 0, 1, 2):
            for d in (4, 5, 2, 6, 3, 1, 7):
                across(d, a, target(d), me).start()

    @pl.when(odd)
    def _():
        for a in range(3):
            for side in range(2):
                hop(side, a).wait_recv()
                passed(side, a).start()

    for a in range(3):
        passed(0, a).wait_recv()

    @pl.when(odd)
    def _():
        for d in range(1, nh):
            for a in range(4):
                if d == 4 and a < 3:
                    continue
                across(d, a, target(d), source(d)).wait_recv()
        for d in range(1, nh):
            for a in range(4):
                if d in (3, 4) and a < 3:
                    continue
                across(d, a, target(d), source(d)).wait_send()
        for a in range(3):
            for side in range(2):
                hop(side, a).wait_send()
                passed(side, a).wait_send()

    @pl.when(jnp.logical_not(odd))
    def _():
        for d in range(1, nh):
            for a in range(4):
                if not (d == 3 and a < 3):
                    across(d, a, target(d), source(d)).wait_recv()
                across(d, a, target(d), source(d)).wait_send()

    @pl.when(seq > 0)
    def _():
        for a in range(3):
            halo(0, a).wait_recv()

    @pl.when(last)
    def _():
        for d in range(nh):
            for a in range(3):
                halo(d, a).wait_send()

    for a in range(4):
        own(a).wait()


VIA = 3


def exchange(ns, nh, arrays):
    rows = arrays[0].shape[0]
    total = rows * nh
    shapes = []
    for i, x in enumerate(arrays):
        width = x.shape[1] // nh if i < 3 else x.shape[1]
        shapes.append(jax.ShapeDtypeStruct((total + (PAD if i < 3 else 0), width), x.dtype))
    return pl.pallas_call(
        functools.partial(exchange_kernel, ns, nh, VIA),
        name="token_exchange",
        out_shape=shapes,
        in_specs=[pl.BlockSpec(memory_space=pl.ANY)] * 4,
        out_specs=[pl.BlockSpec(memory_space=pltpu.VMEM)] * 4,
        scratch_shapes=[pltpu.VMEM((2, rows, s.shape[1]), BF16) for s in shapes[:3]]
        + [
            pltpu.SemaphoreType.DMA((nh - 1, 4)),
            pltpu.SemaphoreType.DMA((nh - 1, 4)),
            pltpu.SemaphoreType.DMA((2, 3)),
            pltpu.SemaphoreType.DMA((2, 3)),
            pltpu.SemaphoreType.DMA((2, 3)),
            pltpu.SemaphoreType.DMA((3,)),
            pltpu.SemaphoreType.DMA((nh, 3)),
            pltpu.SemaphoreType.DMA((3,)),
            pltpu.SemaphoreType.DMA((4,)),
        ],
        compiler_params=pltpu.CompilerParams(
            collective_id=0, has_side_effects=True, vmem_limit_bytes=VMEM_LIMIT
        ),
    )(*arrays)


def local_kernel(
    q_ref, k_ref, v_ref, wl_ref, fq_ref, fk_ref, fv_ref,
    chain_ref, qeff_ref, olocal_ref,
    key_s, query_s, w_s, e_s, mix_s, low_s, flip_s, sol_s, inv_s, value_s,
    grow_s, tail_s, gamma_s, right_s, turned_s, state_s,
):
    seq = lax.axis_index("seq")
    head = lax.axis_index("head")
    tokens = wl_ref.shape[0]
    blocks = tokens // CH
    nheads = v_ref.shape[1] // DV
    nkeys = k_ref.shape[1] // DK
    share = nheads // nkeys
    sets = blocks * nkeys
    both = share * CH
    row = lax.broadcasted_iota(jnp.int32, (CH, both), 0)
    lane = lax.broadcasted_iota(jnp.int32, (CH, both), 1)
    col = lax.rem(lane, CH)
    second_head = lane >= CH
    incl = col <= row
    strict = col < row
    lower_ones = (
        lax.broadcasted_iota(jnp.int32, (CH, CH), 1) <= lax.broadcasted_iota(jnp.int32, (CH, CH), 0)
    ).astype(F32).astype(BF16)
    upper_ones = (row <= col).astype(F32).astype(BF16)
    copies = (row == col).astype(F32).astype(BF16)
    allh = wl_ref.shape[1] // 2
    pick = (
        lax.broadcasted_iota(jnp.int32, (allh, 128), 0)
        == head * nheads + lax.broadcasted_iota(jnp.int32, (allh, 128), 1)
    )
    pick = jnp.logical_and(pick, lax.broadcasted_iota(jnp.int32, (allh, 128), 1) < nheads)
    pick = pick.astype(F32).astype(BF16)
    pick_t = (
        lax.broadcasted_iota(jnp.int32, (8, allh), 1)
        == head * nheads + lax.broadcasted_iota(jnp.int32, (8, allh), 0)
    )
    pick_t = jnp.logical_and(pick_t, lax.broadcasted_iota(jnp.int32, (8, allh), 0) < nheads)
    pick_t = pick_t.astype(F32).astype(BF16)

    def filtered(ref, taps, start, lo, width):
        x = ref[pl.ds(start, CH + PAD), lo : lo + width].astype(F32)
        edge = lax.broadcasted_iota(jnp.int32, (CH + PAD, width), 0) < PAD
        x = jnp.where(jnp.logical_and(edge, jnp.logical_and(seq == 0, start == 0)), 0.0, x)
        total = None
        for j in range(4):
            term = taps[j : j + 1, lo : lo + width].astype(F32) * x[PAD - 3 + j : PAD - 3 + j + CH]
            total = term if total is None else total + term
        return total / (1.0 + jnp.exp(-total))

    def gather_terms(c, carry):
        start = pl.multiple_of(c * CH, CH)
        rows = pl.ds(start, CH)
        wsc = wl_ref[rows, :allh]
        ldc = wl_ref[rows, allh:]
        beta_c = dot(wsc, pick)
        dec_c = dot(ldc, pick)
        beta_r = dot(dot(pick_t, wsc, ((1,), (1,))).astype(BF16), copies)
        dec_r = dot(pick_t, ldc, ((1,), (1,)))
        cum_c = dot(lower_ones, dec_c.astype(BF16))
        cum_r = dot(dec_r.astype(BF16), upper_ones)
        grow_c = jnp.exp(cum_c)
        gamma = grow_c[CH - 1 : CH, :]
        gamma_s[pl.ds(pl.multiple_of(c * 8, 8), 8), :] = jnp.broadcast_to(gamma, (8, 128))
        grow_s[rows, :] = grow_c
        tail_s[pl.ds(pl.multiple_of(c * 8, 8), 8), :] = jnp.exp(cum_r[:, CH - 1 : CH] - cum_r)
        for p in range(nkeys):
            lanes = slice(p * DK, (p + 1) * DK)
            key = filtered(k_ref, fk_ref, start, p * DK, DK)
            key = key * lax.rsqrt(jnp.sum(key * key, axis=1, keepdims=True) + norm_floor)
            query = filtered(q_ref, fq_ref, start, p * DK, DK)
            query = query * (
                lax.rsqrt(jnp.sum(query * query, axis=1, keepdims=True) + norm_floor) * DK ** (-0.5)
            )
            key_s[rows, lanes] = key
            query_s[rows, lanes] = query
            kh, kl = halves(key)
            twice = tuple(jnp.concatenate([t] * share, axis=0) for t in (kh, kl))
            kk = dot3((kh, kl), twice, ((1,), (1,)))
            qk = dot3(halves(query), twice, ((1,), (1,)))
            h = p * share

            at = pl.ds(pl.multiple_of((c * nkeys + p) * CH, CH), CH)
            lowers = []
            for s in range(share):
                spread = cum_c[:, h + s : h + s + 1] - cum_r[h + s : h + s + 1, :]
                ratios = jnp.where(incl, jnp.exp(jnp.where(incl, spread, 0.0)), 0.0)
                mix_s[h + s, rows, :] = qk * ratios
                lowers.append(beta_c[:, h + s : h + s + 1] * kk * ratios)
            low_s[at, :] = jnp.where(strict, jnp.where(second_head, lowers[1], lowers[0]), 0.0)
            turned_s[pl.ds(pl.multiple_of((c * nkeys + p) * DK, DK), DK), :] = jnp.concatenate(
                [key] * share, axis=0
            ).T
            right = jnp.where(second_head[:1], beta_r[h + 1 : h + 2, :], beta_r[h : h + 1, :])
            grown = right * jnp.exp(
                jnp.where(second_head[:1], cum_r[h + 1 : h + 2, :], cum_r[h : h + 1, :])
            )
            right_s[pl.ds(pl.multiple_of((c * nkeys + p) * 8, 8), 8), :] = jnp.concatenate(
                [jnp.broadcast_to(right, (4, both)), jnp.broadcast_to(grown, (4, both))], axis=0
            )
            for s in range(share):
                hv = slice((h + s) * DV, (h + s + 1) * DV)
                value_s[rows, hv] = filtered(v_ref, fv_ref, start, (h + s) * DV, DV)
        return carry

    lax.fori_loop(0, blocks, gather_terms, 0, unroll=2)

    copies_n = 128 // sets
    groups = copies_n // share
    width = CH // groups
    lane_h = lax.rem(lax.broadcasted_iota(jnp.int32, (CH, 128), 1) // sets, share) == 1

    def turn(i, carry):
        x = low_s[pl.ds(i, sets, stride=CH), :]
        t = jnp.concatenate([x] * copies_n, axis=0).T
        flip_s[i] = jnp.where(lane_h, t[CH:], t[:CH])
        return carry

    lax.fori_loop(0, CH, turn, 0, unroll=8)
    place = lax.broadcasted_iota(jnp.int32, (width, 128), 0) + width * (
        lax.broadcasted_iota(jnp.int32, (width, 128), 1) // (sets * share)
    )

    def solve(b, carry):
        base = b * 8
        accs = tuple(jnp.where(place == base + r, 1.0, 0.0) for r in range(8))

        def inner(jb, accs):
            accs = list(accs)
            start = pl.multiple_of(jb * 8, 8)
            tiles = [flip_s[base + r, pl.ds(start, 8), :] for r in range(8)]
            for jj in range(8):
                t = sol_s[start + jj]
                for r in range(8):
                    accs[r] = accs[r] - tiles[r][jj : jj + 1] * t
            return tuple(accs)

        accs = list(lax.fori_loop(0, b, inner, accs))
        tiles = [flip_s[base + r, pl.ds(pl.multiple_of(base, 8), 8), :] for r in range(8)]
        for r in range(8):
            sol_s[base + r] = accs[r]
            for later in range(r + 1, 8):
                accs[later] = accs[later] - tiles[later][r : r + 1] * accs[r]
        return carry

    lax.fori_loop(0, CH // 8, solve, 0)
    from_row = lax.broadcasted_iota(jnp.int32, (128, 128), 0)
    from_lane = lax.broadcasted_iota(jnp.int32, (128, 128), 1)
    matching = jnp.logical_and(
        from_row // CH == lax.rem(from_lane // sets, share),
        lax.rem(from_row, CH) // width == from_lane // (sets * share),
    )

    def turn_back(i, carry):
        x = jnp.where(matching, jnp.concatenate([sol_s[i]] * copies_n, axis=0), 0.0).T
        total = x[:sets]
        for r in range(1, copies_n):
            total = total + x[r * sets : (r + 1) * sets]
        inv_s[pl.ds(i, sets, stride=CH), :] = total
        return carry

    lax.fori_loop(0, CH, turn_back, 0, unroll=8)

    def applied(c, carry):
        rows = pl.ds(pl.multiple_of(c * CH, CH), CH)
        for p in range(nkeys):
            at = pl.ds(pl.multiple_of((c * nkeys + p) * CH, CH), CH)
            inv = inv_s[at, :]
            right = right_s[pl.ds(pl.multiple_of((c * nkeys + p) * 8, 8), 8), :]
            h = p * share
            for source, out, r in ((value_s, w_s, 0), (key_s, e_s, 4)):
                left = halves(inv * right[r : r + 1, :])
                if r == 0:
                    parts = [halves(source[rows, (h + s) * DV : (h + s + 1) * DV]) for s in range(share)]
                else:
                    parts = [halves(source[rows, p * DK : (p + 1) * DK])] * share
                zero = jnp.zeros((CH, DV), BF16)
                wide = tuple(
                    jnp.concatenate(
                        [
                            jnp.concatenate([parts[0][i], zero], axis=1),
                            jnp.concatenate([zero, parts[1][i]], axis=1),
                        ],
                        axis=0,
                    )
                    for i in range(2)
                )
                out[rows, h * DV : (h + share) * DV] = dot3(left, wide)
        return carry

    lax.fori_loop(0, blocks, applied, 0, unroll=4)

    eye_k = (
        lax.broadcasted_iota(jnp.int32, (DK, DK + DV), 0)
        == lax.broadcasted_iota(jnp.int32, (DK, DK + DV), 1)
    ).astype(F32)
    for h in range(nheads):
        state_s[h] = eye_k

    def second(c, carry):
        start = pl.multiple_of(c * CH, CH)
        rows = pl.ds(start, CH)
        grow_c = grow_s[rows, :]
        tail_r = tail_s[pl.ds(pl.multiple_of(c * 8, 8), 8), :]
        gamma = gamma_s[pl.ds(pl.multiple_of(c * 8, 8), 8), :]
        for h in range(nheads):
            p = h // share
            query = query_s[rows, p * DK : (p + 1) * DK]
            state = state_s[h]
            sh, sl = halves(state)
            e = e_s[rows, h * DK : (h + 1) * DK]
            w = w_s[rows, h * DV : (h + 1) * DV]
            lh, ll = halves(jnp.concatenate([e, query * grow_c[:, h : h + 1]], axis=0))
            x = dot(
                jnp.concatenate([lh, ll], axis=1), jnp.concatenate([sh, sh], axis=0)
            ) + dot(lh, sl)
            fresh = jnp.concatenate([-x[:CH, :DK], w - x[:CH, DK:]], axis=1)
            fr = halves(fresh)
            turned = turned_s[pl.ds(pl.multiple_of((c * nkeys + p) * DK, DK), DK), :]
            left = jnp.concatenate([mix_s[h, rows, :], turned * tail_r[h : h + 1, :]], axis=0)
            y = dot(jnp.concatenate(halves(left), axis=1), jnp.concatenate(fr + fr, axis=0))
            state_s[h] = gamma[0:1, h : h + 1] * state + y[CH:]
            y = x[CH:] + y[:CH]
            qeff_ref[rows, h * DK : (h + 1) * DK] = y[:, :DK]
            olocal_ref[rows, h * DV : (h + 1) * DV] = y[:, DK:]
        return carry

    lax.fori_loop(0, blocks, second, 0, unroll=4)
    for h in range(nheads):
        for part in range(2):
            t = state_s[h, :, part * DK : (part + 1) * DK].T
            for r in range(DK // ROWS):
                chain_ref[h * 2 * (DK // ROWS) + part * (DK // ROWS) + r] = t[
                    r * ROWS : (r + 1) * ROWS
                ]


def local_terms(q, k, v, wl, fq, fk, fv):
    tokens = wl.shape[0]
    nheads = v.shape[1] // DV
    nkeys = k.shape[1] // DK
    vm = pl.BlockSpec(memory_space=pltpu.VMEM)
    return pl.pallas_call(
        local_kernel,
        name="local_terms",
        out_shape=[
            jax.ShapeDtypeStruct((nheads * 2 * DK // ROWS, ROWS, DK), F32),
            jax.ShapeDtypeStruct((tokens, nheads * DK), F32),
            jax.ShapeDtypeStruct((tokens, nheads * DV), F32),
        ],
        in_specs=[vm] * 7,
        out_specs=[vm] * 3,
        scratch_shapes=[
            pltpu.VMEM((tokens, nkeys * DK), F32),
            pltpu.VMEM((tokens, nkeys * DK), F32),
            pltpu.VMEM((tokens, nheads * DV), F32),
            pltpu.VMEM((tokens, nheads * DK), F32),
            pltpu.VMEM((nheads, tokens, 2 * CH), F32),
            pltpu.VMEM((tokens * nkeys, 2 * CH), F32),
            pltpu.VMEM((CH, CH, 128), F32),
            pltpu.VMEM((CH, 16, 128), F32),
            pltpu.VMEM((tokens * nkeys, 2 * CH), F32),
            pltpu.VMEM((tokens, nheads * DV), F32),
            pltpu.VMEM((tokens, 128), F32),
            pltpu.VMEM((tokens // CH * 8, 128), F32),
            pltpu.VMEM((tokens // CH * 8, 128), F32),
            pltpu.VMEM((tokens // CH * nkeys * 8, 2 * CH), F32),
            pltpu.VMEM((tokens // CH * nkeys * DK, 2 * CH), F32),
            pltpu.VMEM((nheads, DK, DK + DV), F32),
        ],
        compiler_params=pltpu.CompilerParams(vmem_limit_bytes=VMEM_LIMIT),
    )(q, k, v, wl, fq, fk, fv)


def chain_kernel(
    ns, nh, nz, own_ref, gate_in, entry_ref, gate_ref,
    before, here, map_h, map_l, pre_h, pre_l, tot_h, tot_l, earlier, later,
    pre_send, pre_recv, far_send, far_recv, relay_send, relay_two, gate_send, gate_recv, gate_own,
):
    seq = lax.axis_index("seq")
    head = lax.axis_index("head")
    ny = ns // nz
    z = lax.rem(seq, nz)
    y = seq // nz
    pieces = own_ref.shape[0]
    per_head = 2 * DK // ROWS
    half = per_head // 2
    nheads = pieces // per_head
    npe = nheads * half
    base = y * nz
    up = base + lax.rem(z + 1, nz)
    down = base + lax.rem(z + nz - 1, nz)
    mid = nz // 2
    is_end = z == nz - 1
    rows = gate_in.shape[0]
    width = gate_ref.shape[1]

    barrier = pltpu.get_barrier_semaphore()
    for other in (up, down):
        pl.semaphore_signal(barrier, inc=1, device_id=(other, head), device_id_type=MESH)
    for d in range(1, nh):
        pl.semaphore_signal(
            barrier, inc=1, device_id=(seq, lax.rem(head + d, nh)), device_id_type=MESH
        )

    @pl.when(jnp.logical_and(is_end, y > 0))
    def _():
        pl.semaphore_signal(barrier, inc=1, device_id=(seq - nz, head), device_id_type=MESH)

    @pl.when(jnp.logical_and(is_end, y < ny - 1))
    def _():
        pl.semaphore_signal(barrier, inc=1, device_id=(seq + nz, head), device_id_type=MESH)

    def gate_piece(who):
        return gate_in.at[:, pl.ds(pl.multiple_of(who * width, width), width)]

    def gate_place(who):
        return gate_ref.at[pl.ds(pl.multiple_of(who * rows, 16), rows), :]

    def gate_across(d, to, source):
        return pltpu.make_async_remote_copy(
            src_ref=gate_piece(to),
            dst_ref=gate_place(source),
            send_sem=gate_send.at[d - 1],
            recv_sem=gate_recv.at[d - 1],
            device_id=(seq, to),
            device_id_type=MESH,
        )

    gate_mine = pltpu.make_async_copy(gate_piece(head), gate_place(head), gate_own)
    gate_mine.start()
    for h in range(nheads):
        for r in range(half):
            hi, lo = halves(own_ref[h * per_head + r])
            map_h[h, r * ROWS : (r + 1) * ROWS, :] = hi
            map_l[h, r * ROWS : (r + 1) * ROWS, :] = lo
    pl.semaphore_wait(
        barrier,
        1
        + nh
        + jnp.where(jnp.logical_and(is_end, y > 0), 1, 0)
        + jnp.where(jnp.logical_and(is_end, y < ny - 1), 1, 0),
    )

    def onward(n, source):
        return pltpu.make_async_remote_copy(
            src_ref=source.at[n],
            dst_ref=before.at[n],
            send_sem=pre_send.at[n],
            recv_sem=pre_recv.at[n],
            device_id=(up, head),
            device_id_type=MESH,
        )

    def to_group(m, source):
        return pltpu.make_async_remote_copy(
            src_ref=source.at[m],
            dst_ref=earlier.at[m],
            send_sem=far_send.at[m],
            recv_sem=far_recv.at[m],
            device_id=(seq + nz, head),
            device_id_type=MESH,
        )

    def relay(m, to, sem):
        return pltpu.make_async_remote_copy(
            src_ref=earlier.at[m],
            dst_ref=earlier.at[m],
            send_sem=sem.at[m],
            recv_sem=far_recv.at[m],
            device_id=(to, head),
            device_id_type=MESH,
        )

    @pl.when(z == 0)
    def _():
        def send(n, c):
            onward(n, own_ref).start()
            return c

        lax.fori_loop(0, pieces, send, 0)

    for d in range(1, nh):
        gate_across(d, lax.rem(head + d, nh), head).start()

    def prefix(h, part):
        n = h * per_head + part
        onward(n, here).wait_recv()
        xh, xl = halves(before[n])
        if part < half:
            pre_h[h, part * ROWS : (part + 1) * ROWS, :] = xh
            pre_l[h, part * ROWS : (part + 1) * ROWS, :] = xl
        r = dot3((xh, xl), (map_h[h], map_l[h]))
        if part >= half:
            r = r + own_ref[n]
        here[n] = r

    def corrected(m, h, r):
        entry_ref[m] = (
            dot3(halves(earlier[m]), (pre_h[h], pre_l[h])) + before[h * per_head + half + r]
        )

    @pl.when(jnp.logical_and(z > 0, z < nz - 1))
    def _():
        def step(h, c):
            for part in range(per_head):
                prefix(h, part)
                onward(h * per_head + part, here).start()
            return c

        lax.fori_loop(0, nheads, step, 0)

    @pl.when(is_end)
    def _():
        def step(h, c):
            for part in range(per_head):
                prefix(h, part)

            @pl.when(y == 0)
            def _():
                for r in range(half):
                    m = h * half + r
                    later[m] = here[h * per_head + half + r]
                    to_group(m, later).start()

            @pl.when(y > 0)
            def _():
                for r in range(half):
                    hi, lo = halves(here[h * per_head + r])
                    tot_h[h, r * ROWS : (r + 1) * ROWS, :] = hi
                    tot_l[h, r * ROWS : (r + 1) * ROWS, :] = lo
                for r in range(half):
                    m = h * half + r
                    to_group(m, later).wait_recv()
                    relay(m, down, relay_send).start()
                    relay(m, up, relay_two).start()

                    @pl.when(y < ny - 1)
                    def _():
                        later[m] = (
                            dot3(halves(earlier[m]), (tot_h[h], tot_l[h]))
                            + here[h * per_head + half + r]
                        )
                        to_group(m, later).start()

                for r in range(half):
                    corrected(h * half + r, h, r)

            return c

        lax.fori_loop(0, nheads, step, 0)

    @pl.when(jnp.logical_and(jnp.logical_not(is_end), y > 0))
    def _():
        def step(h, c):
            for r in range(half):
                m = h * half + r
                relay(m, down, relay_send).wait_recv()

                @pl.when(z > mid)
                def _():
                    relay(m, down, relay_send).start()

                @pl.when(z < mid - 1)
                def _():
                    relay(m, up, relay_two).start()

                @pl.when(z == 0)
                def _():
                    entry_ref[m] = earlier[m]

                @pl.when(z > 0)
                def _():
                    corrected(m, h, r)

            return c

        lax.fori_loop(0, nheads, step, 0)

    @pl.when(y == 0)
    def _():
        @pl.when(z == 0)
        def _():
            entry_ref[...] = jnp.zeros_like(entry_ref)

        @pl.when(z > 0)
        def _():
            for m in range(npe):
                entry_ref[m] = before[(m // half) * per_head + half + m % half]

    @pl.when(z < nz - 1)
    def _():
        def done(n, c):
            onward(n, own_ref).wait_send()
            return c

        lax.fori_loop(0, pieces, done, 0)

    @pl.when(jnp.logical_and(is_end, y < ny - 1))
    def _():
        def done(m, c):
            to_group(m, later).wait_send()
            return c

        lax.fori_loop(0, npe, done, 0)

    @pl.when(jnp.logical_and(y > 0, z > mid))
    def _():
        def done(m, c):
            relay(m, down, relay_send).wait_send()
            return c

        lax.fori_loop(0, npe, done, 0)

    @pl.when(jnp.logical_and(y > 0, jnp.logical_or(is_end, z < mid - 1)))
    def _():
        def done(m, c):
            relay(m, up, relay_two).wait_send()
            return c

        lax.fori_loop(0, npe, done, 0)

    gate_mine.wait()
    for d in range(1, nh):
        gate_across(d, lax.rem(head + d, nh), lax.rem(head + nh - d, nh)).wait()


def state_chain(ns, nh, nz, own, gate):
    pieces = own.shape[0]
    nheads = pieces * ROWS // (2 * DK)
    npe = pieces // 2
    vm = pl.BlockSpec(memory_space=pltpu.VMEM)
    return pl.pallas_call(
        functools.partial(chain_kernel, ns, nh, nz),
        name="state_chain",
        out_shape=[
            jax.ShapeDtypeStruct((npe, ROWS, DK), F32),
            jax.ShapeDtypeStruct((gate.shape[0] * nh, gate.shape[1] // nh), gate.dtype),
        ],
        in_specs=[vm, pl.BlockSpec(memory_space=pl.ANY)],
        out_specs=[vm, vm],
        scratch_shapes=[pltpu.VMEM((pieces, ROWS, DK), F32)] * 2
        + [pltpu.VMEM((nheads, DK, DK), BF16)] * 6
        + [pltpu.VMEM((npe, ROWS, DK), F32)] * 2
        + [pltpu.SemaphoreType.DMA((pieces,))] * 2
        + [pltpu.SemaphoreType.DMA((npe,))] * 4
        + [pltpu.SemaphoreType.DMA((nh - 1,))] * 2
        + [pltpu.SemaphoreType.DMA],
        compiler_params=pltpu.CompilerParams(
            collective_id=1, has_side_effects=True, vmem_limit_bytes=VMEM_LIMIT
        ),
    )(own, gate)


def output_kernel(
    nh, qeff_ref, olocal_ref, entry_ref, gate_ref, gain_ref, weight_ref, out_ref,
    normed_s, own_s, twin_out, twin_in, gone, landed, twin_send, twin_recv, send_sem, recv_sem,
):
    seq = lax.axis_index("seq")
    me = lax.axis_index("head")
    nheads = qeff_ref.shape[1] // DK
    chips = nh // 2
    chip = me // 2
    core = lax.rem(me, 2)
    other = 1 - core
    rows = out_ref.shape[0]
    ahead = lax.rem(chip + 1 + 2 * core, chips)
    behind = lax.rem(chip + 3 + 2 * core, chips)
    fwd = 1 + 2 * core
    bwd = 3 - 2 * core
    barrier = pltpu.get_barrier_semaphore()
    pl.semaphore_signal(barrier, inc=1, device_id=(seq, chip * 2 + other), device_id_type=MESH)
    for to in (ahead, behind):
        pl.semaphore_signal(barrier, inc=1, device_id=(seq, to * 2 + core), device_id_type=MESH)

    pieces = DV // ROWS
    entries = []
    for h in range(nheads):
        entry = jnp.concatenate([entry_ref[h * pieces + r] for r in range(pieces)], axis=0)
        entries.append(halves(entry))

    def normalized(d):
        start = pl.multiple_of(lax.rem(chip + d, chips) * (2 * rows), 2 * rows)
        at = pl.ds(start, 2 * rows)
        for h in range(nheads):
            lanes = slice(h * DV, (h + 1) * DV)
            core_out = olocal_ref[at, lanes] + dot3(
                halves(qeff_ref[at, lanes]), entries[h], ((1,), (1,))
            )
            scale = lax.rsqrt(jnp.mean(core_out * core_out, axis=1, keepdims=True) + norm_floor)
            gate = gate_ref[at, lanes].astype(F32)
            gate = gate / (1.0 + jnp.exp(-gate))
            normed_s[:, lanes] = (core_out * scale * gain_ref[...] * gate).astype(BF16)

    def to_twin(d):
        return pltpu.make_async_remote_copy(
            src_ref=twin_out.at[d],
            dst_ref=twin_in.at[d],
            send_sem=twin_send.at[d],
            recv_sem=twin_recv.at[d],
            device_id=(seq, chip * 2 + other),
            device_id_type=MESH,
        )

    def away(i, to):
        return pltpu.make_async_remote_copy(
            src_ref=gone.at[i],
            dst_ref=landed.at[i],
            send_sem=send_sem.at[i],
            recv_sem=recv_sem.at[i],
            device_id=(seq, to * 2 + core),
            device_id_type=MESH,
        )

    wide = 512
    nwide = weight_ref.shape[1] // wide
    mine_at = pl.ds(pl.multiple_of(core * rows, rows), rows)
    other_at = pl.ds(pl.multiple_of(other * rows, rows), rows)

    def project(d):
        normalized(d)
        for j in range(nwide):
            lanes = slice(j * wide, (j + 1) * wide)
            twin_out[d, :, lanes] = dot(normed_s[other_at, :], weight_ref[:, lanes]).astype(BF16)
            own_s[d, :, lanes] = dot(normed_s[mine_at, :], weight_ref[:, lanes])

    def pair_sum(d):
        return own_s[d] + twin_in[d].astype(F32)

    order = (2, 1, 3, 0)
    for i, d in enumerate(order):
        project(d)
        if i == 0:
            pl.semaphore_wait(barrier, 3)
        to_twin(d).start()
        if d == 1:
            to_twin(2).wait_recv()
            gone[0] = pair_sum(2).astype(BF16)
            away(0, ahead).start()
        if d == 3:
            to_twin(1).wait_recv()
        if d == 0:
            to_twin(3).wait_recv()
            gone[2] = pair_sum(bwd).astype(BF16)
            away(2, behind).start()
    away(0, ahead).wait_recv()
    gone[1] = (pair_sum(fwd) + landed[0].astype(F32)).astype(BF16)
    away(1, ahead).start()
    to_twin(0).wait_recv()
    total = pair_sum(0)
    away(2, behind).wait_recv()
    total = total + landed[2].astype(F32)
    away(1, ahead).wait_recv()
    out_ref[...] = (total + landed[1].astype(F32)).astype(BF16)
    for d in order:
        to_twin(d).wait_send()
    for i in range(3):
        away(i, ahead).wait_send()


def output_part(nh, qeff, olocal, entry, gate, gain, weight):
    vm = pl.BlockSpec(memory_space=pltpu.VMEM)
    rows = qeff.shape[0] // nh
    width = weight.shape[1]
    chips = nh // 2
    return pl.pallas_call(
        functools.partial(output_kernel, nh),
        name="gated_projection",
        out_shape=jax.ShapeDtypeStruct((rows, width), BF16),
        in_specs=[vm] * 6,
        out_specs=vm,
        scratch_shapes=[
            pltpu.VMEM((2 * rows, weight.shape[0]), BF16),
            pltpu.VMEM((chips, rows, width), F32),
            pltpu.VMEM((chips, rows, width), BF16),
            pltpu.VMEM((chips, rows, width), BF16),
            pltpu.VMEM((3, rows, width), BF16),
            pltpu.VMEM((3, rows, width), BF16),
            pltpu.SemaphoreType.DMA((chips,)),
            pltpu.SemaphoreType.DMA((chips,)),
            pltpu.SemaphoreType.DMA((3,)),
            pltpu.SemaphoreType.DMA((3,)),
        ],
        compiler_params=pltpu.CompilerParams(
            collective_id=2, has_side_effects=True, vmem_limit_bytes=VMEM_LIMIT
        ),
    )(qeff, olocal, entry, gate, gain, weight)


def on_device(
    ns, nh, query_input, key_input, value_input, gate_input, write_strength, log_decay,
    filter_query, filter_key, filter_value, norm_gain, out_weight,
):
    small = jnp.concatenate([write_strength, log_decay], axis=1)
    q, k, v, wl = exchange(ns, nh, (query_input, key_input, value_input, small))
    own, qeff, olocal = local_terms(q, k, v, wl, filter_query, filter_key, filter_value)
    entry, gate = state_chain(ns, nh, NZ, own, gate_input)
    return output_part(nh, qeff, olocal, entry, gate, norm_gain.reshape(1, DV), out_weight)


def solution(mesh):
    placed = (
        P(("seq", "head"), None),
        P(("seq", "head"), None),
        P(("seq", "head"), None),
        P(("seq", "head"), None),
        P(("seq", "head"), None),
        P(("seq", "head"), None),
        P(None, "head"),
        P(None, "head"),
        P(None, "head"),
        P(),
        P("head", None),
    )
    return jax.shard_map(
        functools.partial(on_device, mesh.shape["seq"], mesh.shape["head"]),
        mesh=mesh,
        in_specs=placed,
        out_specs=P(("seq", "head"), None),
        check_vma=False,
    )
```
